512 devices in a mesh: occ: 16 (over x, y_hi, core), virt: 32 (over y_lo, z).
Axes of the slice: x: 4, y: 4 (y_hi: 2, y_lo: 2; y = y_hi * 2 + y_lo), z: 16, core: 2. Of those that a mesh axis runs over, the one named last changes fastest.
Arguments:
- integrals: bfloat16 [192, 1024, 2048], P('occ', 'virt'), may hold values from -1 to 1
- occ_energy: float32 [192], replicated, may hold values from -2 to -0.5
- virt_energy: float32 [1024], replicated, may hold values from 0.2 to 3
- partners: int32 [2], replicated, may hold values from 0 to 191
Outputs:
- gamma: bfloat16 [192, 1024, 2048], P('occ', 'virt')
The draws below stay inside these ranges and needn't reach their ends.
All inputs are finite; a program needn't handle non-finite values.
Results may differ from the reference program's by a relative error of at most 0.0043.
Values may be sent and summed in bfloat16 or wider, within the bound.
A program may use at most 64 MiB of HBM per device.

```python
import jax
import jax.numpy as jnp
from jax import lax

NV = 1024
NAUX = 2048
STEPS = 2
NOCC = 192


def steps_of(key, shape, shards, least, largest):
    def one(position, blocks):
        draws = jax.random.uniform(jax.random.fold_in(jax.random.fold_in(key, 6), position), (blocks,), jnp.float32, least / len(shards), largest / len(shards))
        return jnp.repeat(jnp.exp(draws), shape[position] // blocks).reshape((-1,) + (1,) * (len(shape) - position - 1))

    factor_of = one(*shards[0])
    for cut in shards[1:]:
        factor_of = factor_of * one(*cut)
    return factor_of


def gaussian(rng, shape, width, reach, split=(), dtype=jnp.bfloat16):
    array = width * jax.random.normal(rng, shape, jnp.float32)
    if split:
        array = array * steps_of(rng, shape, split, -0.22, 0.18)
    return jnp.clip(array, -reach, reach).astype(dtype)


def setup_inputs(seed: int = 0) -> dict:
    keys = jax.random.split(jax.random.key(seed), 5)
    integrals = gaussian(keys[0], (NOCC, NV, NAUX), 0.125, 1.0, ((0, 16), (1, 32)))
    occ_energy = jnp.clip(jax.random.uniform(keys[1], (NOCC,), jnp.float32, -2.0, -0.5), -2.0, -0.5)
    virt_energy = jnp.clip(jax.random.uniform(keys[2], (NV,), jnp.float32, 0.2, 3.0), 0.2, 3.0)
    partners = jax.random.randint(keys[3], (STEPS,), 0, NOCC).astype(jnp.int32)
    return dict(integrals=integrals, occ_energy=occ_energy, virt_energy=virt_energy, partners=partners)


def reference(integrals, occ_energy, virt_energy, partners):
    def one_orbital(inputs):
        occ_block, own_energy = inputs
        total_sum = jnp.zeros(occ_block.shape, jnp.float32)
        for step_index in range(STEPS):
            partner = partners[step_index]
            partner_block = lax.dynamic_index_in_dim(integrals, partner, 0, keepdims=False)
            pair_energy = lax.dynamic_index_in_dim(occ_energy, partner, 0, keepdims=False)
            scores = lax.dot_general(occ_block, partner_block, (((1,), (1,)), ((), ())), preferred_element_type=jnp.float32)
            denominator = virt_energy[:, None] + virt_energy[None, :] - own_energy - pair_energy
            amplitudes = (scores / denominator).astype(jnp.bfloat16)
            total_sum = total_sum + jnp.dot(amplitudes, partner_block, preferred_element_type=jnp.float32)
        return total_sum.astype(jnp.bfloat16)

    return lax.map(one_orbital, (integrals, occ_energy))
```

```python
import jax
import jax.numpy as jnp
from jax import lax
from jax.experimental import pallas as pl
from jax.experimental.pallas import tpu as pltpu
from jax.sharding import PartitionSpec as P

MESH = pl.DeviceIdType.MESH
BF16, F32 = jnp.bfloat16, jnp.float32
NX, NY, NC, NZ = 4, 4, 2, 16
NOCC_AX = 16
LANES = 128
PAIRS = NZ // 2
STAGES = 5


def kernel(
    partners, occ_energy, virt_energy, x_hbm, out_hbm,
    xv, pieces, got, ybuf, acc, outv, va, own, vb,
    x_sem, out_sem, rs_send, rs_recv, z_send, z_recv,
    a_send, a_recv, b_send, b_recv, c_send, c_recv,
):
    occ_dev, local_virt, aux = xv.shape
    rows = occ_dev * local_virt
    o, v = lax.axis_index("occ"), lax.axis_index("virt")
    x, yh, c = o // 4, (o // 2) % 2, o % 2
    yl, z = v // NZ, v % NZ
    y = 2 * yh + yl
    step_dir = 1 - 2 * c

    def at(xx, yy, cc, zz):
        return {"occ": (xx * 2 + yy // 2) * 2 + cc, "virt": (yy % 2) * NZ + zz}

    def send(src, dst, s_sem, r_sem, device):
        return pltpu.make_async_remote_copy(
            src_ref=src, dst_ref=dst, send_sem=s_sem, recv_sem=r_sem,
            device_id=device, device_id_type=MESH,
        )

    def x_at(d):
        return at((x + d + NX) % NX, y, c, z)

    def y_at(d):
        return at(x, (y + d + NY) % NY, c, z)

    def occ_at(j):
        return {"occ": (o + j) % NOCC_AX, "virt": v}

    def z_at(d):
        return at(x, y, c, (z + d + NZ) % NZ)

    barrier = pltpu.get_barrier_semaphore()
    peers = [occ_at(j) for j in range(1, NOCC_AX)]
    peers += [y_at(1), y_at(-1)]
    peers += [z_at(j) for j in range(1, NZ)]
    for peer in peers:
        pl.semaphore_signal(barrier, inc=1, device_id=peer, device_id_type=MESH)

    x_copy = pltpu.make_async_copy(x_hbm, xv, x_sem)
    x_copy.start()

    lane = lax.broadcasted_iota(jnp.int32, (local_virt, LANES), 1)
    sub = lax.broadcasted_iota(jnp.int32, (local_virt, LANES), 0)
    line = jnp.broadcast_to(virt_energy[pl.ds(v // 4, 1), :], (local_virt, LANES))
    mine = jnp.sum(jnp.where(lane == sub + (v % 4) * local_virt, line, 0.0), axis=1, keepdims=True)
    mine = jnp.broadcast_to(mine, (local_virt, LANES))
    for i in range(occ_dev):
        va[pl.ds(i * local_virt, local_virt), :] = mine
        own[pl.ds(i * local_virt, local_virt), :] = jnp.full((local_virt, LANES), occ_energy[o * occ_dev + i], F32)
    lane8 = lax.broadcasted_iota(jnp.int32, (8, LANES), 1)
    for k in range(PAIRS):
        total = jnp.zeros((8, LANES), F32)
        for yy in range(2):
            for sign in range(2):
                zz = (z + NZ - k) % NZ if sign == 0 else (z + k + 1) % NZ
                row = jnp.broadcast_to(virt_energy[pl.ds(yy * 4 + zz // 4, 1), :], (8, LANES))
                place = yy * 64 + sign * 32
                turned = pltpu.roll(row, (place - (zz % 4) * 32 + LANES) % LANES, 1)
                total = jnp.where(lane8 // 32 == yy * 2 + sign, turned, total)
        vb[k] = total

    acc[...] = jnp.zeros_like(acc)
    x_copy.wait()
    for s in range(2):
        block = xv[partners[s] % occ_dev]
        for j in range(NOCC_AX):
            pieces[j, s] = block[:, j * LANES:(j + 1) * LANES]

    pl.semaphore_wait(barrier, len(peers))

    for j in range(1, NOCC_AX):
        to = (o + j) % NOCC_AX
        send(pieces.at[to], got.at[o], rs_send.at[to], rs_recv.at[o], occ_at(j)).start()
    got[o] = pieces[o]
    for j in range(1, NOCC_AX):
        source = (o + j) % NOCC_AX
        send(pieces.at[source], got.at[source], rs_send.at[source], rs_recv.at[source], occ_at(j)).wait_recv()
    for s in range(2):
        ybuf[0, c, s, y, x, 0] = got[partners[s] // occ_dev, s]

    mine_ref = ybuf.at[0, c, :, y, x, 0]

    def z_copy(k, sign, d):
        return send(mine_ref, ybuf.at[k, c, :, y, x, sign], z_send.at[k, sign], z_recv.at[k, sign], z_at(d))

    for j in range(1, PAIRS + 1):
        z_copy(j - 1, 1, -j).start()
        if j < PAIRS:
            z_copy(j, 0, j).start()

    def line_ref(k, phase, s, index):
        if phase == 0:
            return ybuf.at[k, c, 0, y, index] if s == 0 else ybuf.at[k, c, 1, index, x]
        return ybuf.at[k, c, 0, index] if s == 0 else ybuf.at[k, c, 1, :, index]

    def hop(k, phase, s, which):
        along_x = (phase + s) % 2 == 0
        pos, count, device = (x, NX, x_at) if along_x else (y, NY, y_at)
        s_sem, r_sem = (a_send, a_recv) if phase == 0 else (b_send, b_recv)
        if which == 2:
            ref = line_ref(k, phase, s, (pos - step_dir + count) % count)
            target = device(step_dir)
        else:
            ref = line_ref(k, phase, s, pos)
            target = device(1 - 2 * which)
        return send(ref, ref, s_sem.at[k, s, which], r_sem.at[k, s, which], target)

    def wait_hop(k, phase, s, which):
        along_x = (phase + s) % 2 == 0
        ref = line_ref(k, phase, s, x if along_x else y)
        s_sem, r_sem = (a_send, a_recv) if phase == 0 else (b_send, b_recv)
        send(ref, ref, s_sem.at[k, s, which], r_sem.at[k, s, which], x_at(1)).wait_recv()

    def twin(k):
        ref = ybuf.at[k, c]
        return send(ref, ref, c_send.at[k], c_recv.at[k], at(x, y, 1 - c, z))

    def first(k):
        @pl.when(k > 0)
        def _():
            z_copy(k, 0, 1).wait_recv()

        z_copy(k, 1, 1).wait_recv()
        for s in range(2):
            hop(k, 0, s, 0).start()
            hop(k, 0, s, 1).start()

    def second(k, phase):
        for s in range(2):
            wait_hop(k, phase, s, c)
            hop(k, phase, s, 2).start()

    def third(k):
        for s in range(2):
            wait_hop(k, 0, s, 1 - c)
            wait_hop(k, 0, s, 2)
            hop(k, 1, s, 0).start()
            hop(k, 1, s, 1).start()

    def fifth(k):
        for s in range(2):
            wait_hop(k, 1, s, 1 - c)
            wait_hop(k, 1, s, 2)
        twin(k).start()

    def tile(k, t):
        parts = []
        for s in range(2):
            for yy in range(2):
                halves = []
                for cc in range(2):
                    block = ybuf[k, cc, s, 2 * (t % 2) + yy, t // 2]
                    halves.append(block.reshape(2 * local_virt, LANES))
                parts.append(jnp.concatenate(halves, axis=1))
        return jnp.concatenate(parts, axis=0)

    def contract(k):
        scores = jnp.zeros((rows, 2 * LANES), F32)
        for t in range(aux // 256):
            left = xv[:, :, t * 256:(t + 1) * 256].reshape(rows, 256)
            scores += lax.dot_general(left, tile(k, t), (((1,), (1,)), ((), ())), preferred_element_type=F32)
        base = va[...] + vb[k][0:1, :] - own[...]
        amplitudes = jnp.concatenate(
            [
                (scores[:, s * LANES:(s + 1) * LANES] / (base - occ_energy[partners[s]])).astype(BF16)
                for s in range(2)
            ],
            axis=1,
        )
        for t in range(aux // 256):
            acc[:, t * 256:(t + 1) * 256] += jnp.dot(amplitudes, tile(k, t), preferred_element_type=F32)

    def sixth(k):
        send(ybuf.at[k, c], ybuf.at[k, 1 - c], c_send.at[k], c_recv.at[k], at(x, y, 1 - c, z)).wait_recv()
        contract(k)

    def tick(t, carry):
        def when(lag, run):
            @pl.when(jnp.logical_and(t >= lag, t < PAIRS + lag))
            def _():
                run(t - lag)

        when(4, fifth)
        when(3, lambda k: second(k, 1))
        when(2, third)
        when(1, lambda k: second(k, 0))
        when(0, first)
        when(5, sixth)
        return carry

    lax.fori_loop(0, PAIRS + STAGES, tick, 0)

    copies = []
    for t in range(aux // 512):
        cols = pl.ds(t * 512, 512)
        outv[:, :, cols] = acc[:, t * 512:(t + 1) * 512].reshape(occ_dev, local_virt, 512).astype(BF16)
        copy = pltpu.make_async_copy(outv.at[:, :, cols], out_hbm.at[:, :, cols], out_sem.at[t])
        copy.start()
        copies.append(copy)

    for j in range(1, NOCC_AX):
        to = (o + j) % NOCC_AX
        send(pieces.at[to], got.at[o], rs_send.at[to], rs_recv.at[o], occ_at(j)).wait_send()
    for j in range(1, PAIRS + 1):
        z_copy(j - 1, 1, -j).wait_send()
        if j < PAIRS:
            z_copy(j, 0, j).wait_send()

    def drain(k, carry):
        for phase in range(2):
            for s in range(2):
                for which in range(3):
                    hop(k, phase, s, which).wait_send()
        twin(k).wait_send()
        return carry

    lax.fori_loop(0, PAIRS, drain, 0)
    for copy in copies:
        copy.wait()


def per_device(integrals, occ_energy, virt_energy, partners):
    occ_dev, local_virt, aux = integrals.shape
    rows = occ_dev * local_virt
    dma = pltpu.SemaphoreType.DMA
    return pl.pallas_call(
        kernel,
        out_shape=jax.ShapeDtypeStruct(integrals.shape, BF16),
        in_specs=[
            pl.BlockSpec(memory_space=pltpu.SMEM),
            pl.BlockSpec(memory_space=pltpu.SMEM),
            pl.BlockSpec(memory_space=pltpu.VMEM),
            pl.BlockSpec(memory_space=pl.ANY),
        ],
        out_specs=pl.BlockSpec(memory_space=pl.ANY),
        scratch_shapes=[
            pltpu.VMEM(integrals.shape, BF16),
            pltpu.VMEM((NOCC_AX, 2, local_virt, LANES), BF16),
            pltpu.VMEM((NOCC_AX, 2, local_virt, LANES), BF16),
            pltpu.VMEM((PAIRS, NC, 2, NY, NX, 2, local_virt, LANES), BF16),
            pltpu.VMEM((rows, aux), F32),
            pltpu.VMEM(integrals.shape, BF16),
            pltpu.VMEM((rows, LANES), F32),
            pltpu.VMEM((rows, LANES), F32),
            pltpu.VMEM((PAIRS, 8, LANES), F32),
            dma, dma((aux // 512,)),
            dma((NOCC_AX,)), dma((NOCC_AX,)),
            dma((PAIRS, 2)), dma((PAIRS, 2)),
            dma((PAIRS, 2, 3)), dma((PAIRS, 2, 3)),
            dma((PAIRS, 2, 3)), dma((PAIRS, 2, 3)),
            dma((PAIRS,)), dma((PAIRS,)),
        ],
        compiler_params=pltpu.CompilerParams(collective_id=0, has_side_effects=True),
    )(partners, occ_energy, virt_energy.reshape(8, LANES), integrals)


def solution(mesh):
    in_specs = (P("occ", "virt", None), P(), P(), P())
    return jax.shard_map(
        per_device, mesh=mesh, in_specs=in_specs, out_specs=P("occ", "virt", None), check_vma=False
    )
```

```python
import jax
import jax.numpy as jnp
from jax import lax
from jax.experimental import pallas as pl
from jax.experimental.pallas import tpu as pltpu
from jax.sharding import PartitionSpec as P

MESH = pl.DeviceIdType.MESH
BF16, F32 = jnp.bfloat16, jnp.float32
NX, NY, NC, NZ = 4, 4, 2, 16
NOCC_AX = 16
LANES = 128
PAIRS = NZ // 2
STAGES = 5


def kernel(
    partners, occ_energy, virt_energy, x_hbm, out,
    xv, pieces, got, ybuf, acc, amp, va, own, vb,
    x_sem, rs_send, rs_recv, z_send, z_recv,
    a_send, a_recv, b_send, b_recv, c_send, c_recv,
):
    occ_dev, local_virt, aux = xv.shape
    rows = occ_dev * local_virt
    o, v = lax.axis_index("occ"), lax.axis_index("virt")
    x, yh, c = o // 4, (o // 2) % 2, o % 2
    yl, z = v // NZ, v % NZ
    y = 2 * yh + yl
    step_dir = 1 - 2 * c

    def at(xx, yy, cc, zz):
        return {"occ": (xx * 2 + yy // 2) * 2 + cc, "virt": (yy % 2) * NZ + zz}

    def send(src, dst, s_sem, r_sem, device):
        return pltpu.make_async_remote_copy(
            src_ref=src, dst_ref=dst, send_sem=s_sem, recv_sem=r_sem,
            device_id=device, device_id_type=MESH,
        )

    def x_at(d):
        return at((x + d + NX) % NX, y, c, z)

    def y_at(d):
        return at(x, (y + d + NY) % NY, c, z)

    def occ_at(j):
        return {"occ": (o + j) % NOCC_AX, "virt": v}

    def z_at(d):
        return at(x, y, c, (z + d + NZ) % NZ)

    x_copy = pltpu.make_async_copy(x_hbm, xv, x_sem)
    x_copy.start()

    barrier = pltpu.get_barrier_semaphore()
    peers = [occ_at(j) for j in range(1, NOCC_AX)]
    peers += [y_at(1), y_at(-1)]
    peers += [z_at(j) for j in range(1, NZ)]
    for peer in peers:
        pl.semaphore_signal(barrier, inc=1, device_id=peer, device_id_type=MESH)

    x_copy.wait()
    for s in range(2):
        block = xv[partners[s] % occ_dev]
        for j in range(NOCC_AX):
            pieces[j, s] = block[:, j * LANES:(j + 1) * LANES]

    pl.semaphore_wait(barrier, len(peers))

    for j in range(1, NOCC_AX):
        send(pieces.at[(o + j) % NOCC_AX], got.at[o], rs_send, rs_recv, occ_at(j)).start()
    got[o] = pieces[o]

    lane = lax.broadcasted_iota(jnp.int32, (local_virt, LANES), 1)
    sub = lax.broadcasted_iota(jnp.int32, (local_virt, LANES), 0)
    line = jnp.broadcast_to(virt_energy[pl.ds(v // 4, 1), :], (local_virt, LANES))
    mine = jnp.sum(jnp.where(lane == sub + (v % 4) * local_virt, line, 0.0), axis=1, keepdims=True)
    mine = jnp.broadcast_to(mine, (local_virt, LANES))
    for i in range(occ_dev):
        va[pl.ds(i * local_virt, local_virt), :] = mine
        own[pl.ds(i * local_virt, local_virt), :] = jnp.full((local_virt, LANES), occ_energy[o * occ_dev + i], F32)
    lane8 = lax.broadcasted_iota(jnp.int32, (8, LANES), 1)
    for k in range(PAIRS):
        total = jnp.zeros((8, LANES), F32)
        for yy in range(2):
            for sign in range(2):
                zz = (z + NZ - k) % NZ if sign == 0 else (z + k + 1) % NZ
                row = jnp.broadcast_to(virt_energy[pl.ds(yy * 4 + zz // 4, 1), :], (8, LANES))
                place = yy * 64 + sign * 32
                turned = pltpu.roll(row, (place - (zz % 4) * 32 + LANES) % LANES, 1)
                total = jnp.where(lane8 // 32 == yy * 2 + sign, turned, total)
        vb[k] = total
    acc[...] = jnp.zeros_like(acc)

    others = pieces.at[pl.ds(0, NOCC_AX - 1)]
    send(others, others, rs_send, rs_recv, occ_at(1)).wait_recv()
    for s in range(2):
        ybuf[0, c, s, y, x, 0] = got[partners[s] // occ_dev, s]

    mine_ref = ybuf.at[0, c, :, y, x, 0]

    def z_copy(k, sign, d):
        return send(mine_ref, ybuf.at[k, c, :, y, x, sign], z_send, z_recv.at[k], z_at(d))

    for j in range(1, PAIRS + 1):
        z_copy(j - 1, 1, -j).start()
        if j < PAIRS:
            z_copy(j, 0, j).start()

    def first(k):
        @pl.when(k > 0)
        def _():
            ref = pieces.at[pl.ds(0, 2)]
            send(ref, ref, z_send, z_recv.at[k], z_at(1)).wait_recv()

        @pl.when(k == 0)
        def _():
            ref = pieces.at[0]
            send(ref, ref, z_send, z_recv.at[k], z_at(1)).wait_recv()

        for d in (1, -1, 2):
            for s in range(2):
                ref = ybuf.at[k, c, s, y, x]
                send(ref, ref, a_send, a_recv.at[k], (y_at if s else x_at)(d)).start()

    def whole(k, s, index):
        return ybuf.at[k, c, 1, :, index] if s else ybuf.at[k, c, 0, index]

    def third(k):
        ref = ybuf.at[k, c, 0, pl.ds(0, 3), pl.ds(0, 2)]
        send(ref, ref, a_send, a_recv.at[k], x_at(1)).wait_recv()
        for s in range(2):
            ref = whole(k, s, x if s else y)
            to = x_at if s else y_at
            send(ref, ref, b_send, b_recv.at[k, 0], to(step_dir)).start()
            send(ref, ref, b_send, b_recv.at[k, 1], to(-step_dir)).start()

    def fourth(k):
        ref = ybuf.at[k, c, 0, pl.ds(0, 2)]
        send(ref, ref, b_send, b_recv.at[k, 0], x_at(1)).wait_recv()
        for s in range(2):
            ref = whole(k, s, ((x if s else y) - step_dir + 4) % 4)
            send(ref, ref, b_send, b_recv.at[k, 1], (x_at if s else y_at)(step_dir)).start()

    def fifth(k):
        ref = ybuf.at[k, c, 0]
        send(ref, ref, b_send, b_recv.at[k, 1], x_at(1)).wait_recv()
        ref = ybuf.at[k, c]
        send(ref, ref, c_send, c_recv.at[k], at(x, y, 1 - c, z)).start()

    def tile(k, t):
        parts = []
        for s in range(2):
            for yy in range(2):
                halves = []
                for cc in range(2):
                    block = ybuf[k, cc, s, 2 * (t % 2) + yy, t // 2]
                    halves.append(block.reshape(2 * local_virt, LANES))
                parts.append(jnp.concatenate(halves, axis=1))
        return jnp.concatenate(parts, axis=0)

    def score(k):
        send(ybuf.at[k, c], ybuf.at[k, 1 - c], c_send, c_recv.at[k], at(x, y, 1 - c, z)).wait_recv()
        scores = jnp.zeros((rows, 2 * LANES), F32)
        for t in range(aux // 256):
            left = xv[:, :, t * 256:(t + 1) * 256].reshape(rows, 256)
            scores += lax.dot_general(left, tile(k, t), (((1,), (1,)), ((), ())), preferred_element_type=F32)
        base = va[...] + vb[k][0:1, :] - own[...]
        for s in range(2):
            cols = slice(s * LANES, (s + 1) * LANES)
            amp[:, cols] = (scores[:, cols] / (base - occ_energy[partners[s]])).astype(BF16)

    def collect(k):
        for t in range(aux // 256):
            acc[:, t * 256:(t + 1) * 256] += jnp.dot(amp[...], tile(k, t), preferred_element_type=F32)

    def tick(t, carry):
        def when(lag, run):
            @pl.when(jnp.logical_and(t >= lag, t < PAIRS + lag))
            def _():
                run(t - lag)

        when(2, third)
        when(0, first)
        when(3, fourth)
        when(5, score)
        when(4, fifth)
        when(5, collect)
        return carry

    lax.fori_loop(0, PAIRS + STAGES, tick, 0)

    for t in range(aux // 256):
        cols = slice(t * 256, (t + 1) * 256)
        out[:, :, cols] = acc[:, cols].reshape(occ_dev, local_virt, 256).astype(BF16)

    for ref, sem in (
        (others, rs_send),
        (others, z_send),
        (ybuf.at[pl.ds(0, 3), 0, 0], a_send),
        (ybuf.at[pl.ds(0, 3)], b_send),
        (ybuf.at[pl.ds(0, 4)], c_send),
    ):
        send(ref, ref, sem, rs_recv, x_at(1)).wait_send()


def per_device(integrals, occ_energy, virt_energy, partners):
    occ_dev, local_virt, aux = integrals.shape
    rows = occ_dev * local_virt
    dma = pltpu.SemaphoreType.DMA
    return pl.pallas_call(
        kernel,
        out_shape=pltpu.VMEM(integrals.shape, BF16),
        in_specs=[
            pl.BlockSpec(memory_space=pltpu.SMEM),
            pl.BlockSpec(memory_space=pltpu.SMEM),
            pl.BlockSpec(memory_space=pltpu.VMEM),
            pl.BlockSpec(memory_space=pl.ANY),
        ],
        out_specs=pl.BlockSpec(memory_space=pltpu.VMEM),
        scratch_shapes=[
            pltpu.VMEM(integrals.shape, BF16),
            pltpu.VMEM((NOCC_AX, 2, local_virt, LANES), BF16),
            pltpu.VMEM((NOCC_AX, 2, local_virt, LANES), BF16),
            pltpu.VMEM((PAIRS, NC, 2, NY, NX, 2, local_virt, LANES), BF16),
            pltpu.VMEM((rows, aux), F32),
            pltpu.VMEM((rows, 2 * LANES), BF16),
            pltpu.VMEM((rows, LANES), F32),
            pltpu.VMEM((rows, LANES), F32),
            pltpu.VMEM((PAIRS, 8, LANES), F32),
            dma, dma, dma,
            dma, dma((PAIRS,)),
            dma, dma((PAIRS,)),
            dma, dma((PAIRS, 2)),
            dma, dma((PAIRS,)),
        ],
        compiler_params=pltpu.CompilerParams(collective_id=0, has_side_effects=True),
    )(partners, occ_energy, virt_energy.reshape(8, LANES), integrals)


def solution(mesh):
    in_specs = (P("occ", "virt", None), P(), P(), P())
    return jax.shard_map(
        per_device, mesh=mesh, in_specs=in_specs, out_specs=P("occ", "virt", None), check_vma=False
    )
```

```python
import jax
import jax.numpy as jnp
from jax import lax
from jax.experimental import pallas as pl
from jax.experimental.pallas import tpu as pltpu
from jax.sharding import PartitionSpec as P

MESH = pl.DeviceIdType.MESH
BF16, F32 = jnp.bfloat16, jnp.float32
NX, NY, NC, NZ = 4, 4, 2, 16
NOCC_AX = 16
LANES = 128
DISTANCE = (0, 1, 3, 5, 6, 7, 8, 2, 4)
SLOTS = len(DISTANCE)
LAST = 6


def kernel(
    partners_hbm, occ_hbm, virt_hbm, x_hbm, out,
    partners, occ_energy, virt_energy, xv, pieces, got, ybuf, acc, amp, va, own, vb, vh,
    x_sem, e_sem, rs_send, rs_recv, z_send, z_recv,
    a_send, a_recv, b_send, b_recv, c_send, c_recv, f_send, f_recv,
):
    occ_dev, local_virt, aux = xv.shape
    rows = occ_dev * local_virt
    o, v = lax.axis_index("occ"), lax.axis_index("virt")
    x, yh, c = o // 4, (o // 2) % 2, o % 2
    yl, z = v // NZ, v % NZ
    y = 2 * yh + yl
    step_dir = 1 - 2 * c

    def at(xx, yy, cc, zz):
        return {"occ": (xx * 2 + yy // 2) * 2 + cc, "virt": (yy % 2) * NZ + zz}

    def send(src, dst, s_sem, r_sem, device):
        return pltpu.make_async_remote_copy(
            src_ref=src, dst_ref=dst, send_sem=s_sem, recv_sem=r_sem,
            device_id=device, device_id_type=MESH,
        )

    def x_at(d):
        return at((x + d + NX) % NX, y, c, z)

    def y_at(d):
        return at(x, (y + d + NY) % NY, c, z)

    def member(dx, dyh, dc):
        return (((x + dx) % NX) * 2 + (yh + dyh) % 2) * 2 + (c + dc) % 2

    def z_at(d):
        return at(x, y, c, (z + d + NZ) % NZ)

    copies = [
        pltpu.make_async_copy(partners_hbm, partners, e_sem.at[0]),
        pltpu.make_async_copy(x_hbm, xv, x_sem),
        pltpu.make_async_copy(occ_hbm, occ_energy, e_sem.at[1]),
        pltpu.make_async_copy(virt_hbm, virt_energy, e_sem.at[2]),
    ]
    for copy in copies:
        copy.start()

    barrier = pltpu.get_barrier_semaphore()
    others = [(dx, dyh, dc) for dx, dyh in ((2, 1), (1, 1), (3, 1), (2, 0), (0, 1), (1, 0), (3, 0), (0, 0)) for dc in (0, 1)][:-2] + [(0, 0, 1)]
    peers = [{"occ": member(*d), "virt": v} for d in others[:-1]]
    peers += [z_at(sign * DISTANCE[u]) for u in (3, 2, 1) for sign in (1, -1)]
    peers += [y_at(1), y_at(-1), {"occ": member(0, 0, 1), "virt": v}]
    for peer in peers:
        pl.semaphore_signal(barrier, inc=1, device_id=peer, device_id_type=MESH)

    copies[0].wait()
    copies[1].wait()
    for s in range(2):
        block = xv[partners[s] % occ_dev]
        for j in range(NOCC_AX):
            pieces[j, s] = block[:, j * LANES:(j + 1) * LANES]

    pl.semaphore_wait(barrier, len(peers))

    for d in others:
        send(pieces.at[member(*d)], got.at[o], rs_send, rs_recv, {"occ": member(*d), "virt": v}).start()
    got[o] = pieces[o]

    copies[2].wait()
    copies[3].wait()
    lane = lax.broadcasted_iota(jnp.int32, (local_virt, LANES), 1)
    sub = lax.broadcasted_iota(jnp.int32, (local_virt, LANES), 0)
    line = jnp.broadcast_to(virt_energy[pl.ds(v // 4, 1), :], (local_virt, LANES))
    mine = jnp.sum(jnp.where(lane == sub + (v % 4) * local_virt, line, 0.0), axis=1, keepdims=True)
    mine = jnp.broadcast_to(mine, (local_virt, LANES))
    for i in range(occ_dev):
        va[pl.ds(i * local_virt, local_virt), :] = mine
        own[pl.ds(i * local_virt, local_virt), :] = jnp.full((local_virt, LANES), occ_energy[o * occ_dev + i], F32)
    lane8 = lax.broadcasted_iota(jnp.int32, (8, LANES), 1) // 32

    def turned(yy, zz, slot):
        row = jnp.broadcast_to(virt_energy[pl.ds(yy * 4 + zz // 4, 1), :], (8, LANES))
        return pltpu.roll(row, ((slot - zz % 4 + 4) % 4) * 32, 1)

    for u, d in enumerate(DISTANCE):
        if d in (0, NZ // 2):
            continue
        total = jnp.zeros((8, LANES), F32)
        for yy in range(2):
            for sign in range(2):
                zz = (z + d) % NZ if sign else (z + NZ - d) % NZ
                total = jnp.where(lane8 == yy * 2 + sign, turned(yy, zz, yy * 2 + sign), total)
        vb[u] = total
    for h in range(2):
        total = jnp.zeros((8, LANES), F32)
        for s in range(2):
            for yy in range(2):
                total = jnp.where(lane8 == s * 2 + yy, turned(yy, (z + 8 * h) % NZ, s * 2 + yy), total)
        vh[h] = total
    acc[...] = jnp.zeros_like(acc)

    fifteen = pieces.at[pl.ds(0, NOCC_AX - 1)]
    send(fifteen, fifteen, rs_send, rs_recv, x_at(1)).wait_recv()
    for s in range(2):
        ybuf[0, c, s, y, x, 0] = got[partners[s] // occ_dev, s]

    def z_copy(u, source, to, sign, d):
        return send(
            ybuf.at[u, c, :, y, x, source], ybuf.at[to, c, :, y, x, sign], z_send, z_recv.at[to], z_at(d)
        )

    def first(u, half):
        if half:
            @pl.when(u > 0)
            def _():
                ref = pieces.at[0]
                send(ref, ref, z_send, z_recv.at[u], z_at(1)).wait_recv()
        else:
            ref = pieces.at[pl.ds(0, 2)]
            send(ref, ref, z_send, z_recv.at[u], z_at(1)).wait_recv()

            @pl.when(u >= 3)
            def _():
                z_copy(u, 0, u + 1, 0, 1).start()

            @pl.when(jnp.logical_and(u >= 3, u < LAST - 1))
            def _():
                z_copy(u, 1, u + 1, 1, -1).start()

        for d in (1, -1, 2):
            for s in range(2):
                ref = ybuf.at[u, c, s, y, x, 0] if half else ybuf.at[u, c, s, y, x]
                send(ref, ref, a_send, a_recv.at[u], (y_at if s else x_at)(d)).start()

    def whole(u, half, s, index):
        if half:
            return ybuf.at[u, c, 1, :, index, 0] if s else ybuf.at[u, c, 0, index, :, 0]
        return ybuf.at[u, c, 1, :, index] if s else ybuf.at[u, c, 0, index]

    def third(u, half):
        six = ybuf.at[0, 0, 0, pl.ds(0, 3), pl.ds(0, 2), 0] if half else ybuf.at[0, 0, 0, pl.ds(0, 3), pl.ds(0, 2)]
        send(six, six, a_send, a_recv.at[u], x_at(1)).wait_recv()
        for s in range(2):
            ref = whole(u, half, s, x if s else y)
            to = x_at if s else y_at
            send(ref, ref, b_send, b_recv.at[u, 0], to(step_dir)).start()
            send(ref, ref, b_send, b_recv.at[u, 1], to(-step_dir)).start()

    def fourth(u, half):
        eight = ybuf.at[0, 0, 0, pl.ds(0, 2), :, 0] if half else ybuf.at[0, 0, 0, pl.ds(0, 2)]
        send(eight, eight, b_send, b_recv.at[u, 0], x_at(1)).wait_recv()
        for s in range(2):
            ref = whole(u, half, s, ((x if s else y) - step_dir + 4) % 4)
            send(ref, ref, b_send, b_recv.at[u, 1], (x_at if s else y_at)(step_dir)).start()

    def twin(u, half, core):
        ref = ybuf.at[u, core, :, :, :, 0] if half else ybuf.at[u, core]
        return send(ref, ref, c_send, c_recv.at[u], at(x, y, 1 - c, z))

    def fifth(u, half):
        sixteen = ybuf.at[0, 0, 0, :, :, 0] if half else ybuf.at[0, 0, 0]
        send(sixteen, sixteen, b_send, b_recv.at[u, 1], x_at(1)).wait_recv()
        twin(u, half, c).start()
        if not half:
            @pl.when(u < 3)
            def _():
                for sign in range(2):
                    send(
                        ybuf.at[u, c, :, :, :, sign], ybuf.at[u + LAST, c, :, :, :, sign],
                        f_send, f_recv.at[u], z_at(1 - 2 * sign),
                    ).start()

    def passed(u):
        send(ybuf.at[0, 0], ybuf.at[0, 0], f_send, f_recv.at[u - LAST], z_at(1)).wait_recv()
        twin(u, False, c).start()

    def tile(u, half, t):
        parts = []
        for s in range(2):
            for yy in range(2):
                halves = []
                for cc in range(2):
                    if half:
                        halves.append(ybuf[u, cc, s, 2 * (t % 2) + yy, t // 2, 0])
                    else:
                        halves.append(ybuf[u, cc, s, 2 * (t % 2) + yy, t // 2].reshape(2 * local_virt, LANES))
                parts.append(jnp.concatenate(halves, axis=1))
        return jnp.concatenate(parts, axis=0)

    def score(u, half):
        twin(u, half, 1 - c).wait_recv()
        width = LANES if half else 2 * LANES
        scores = jnp.zeros((rows, width), F32)
        for t in range(aux // 256):
            left = xv[:, :, t * 256:(t + 1) * 256].reshape(rows, 256)
            scores += lax.dot_general(left, tile(u, half, t), (((1,), (1,)), ((), ())), preferred_element_type=F32)
        line = vh[u // LAST] if half else vb[u]
        base = va[...] + line[0:1, :] - own[...]
        pair = [occ_energy[partners[s]] for s in range(2)]
        if half:
            both = jnp.where(lax.broadcasted_iota(jnp.int32, (1, LANES), 1) < 64, pair[0], pair[1])
            amp[:, :LANES] = (scores / (base - both)).astype(BF16)
        else:
            for s in range(2):
                cols = slice(s * LANES, (s + 1) * LANES)
                amp[:, cols] = (scores[:, cols] / (base - pair[s])).astype(BF16)

    def collect(u, half):
        for t in range(aux // 256):
            cols = slice(t * 256, (t + 1) * 256)
            left = amp[:, :LANES] if half else amp[...]
            acc[:, cols] += jnp.dot(left, tile(u, half, t), preferred_element_type=F32)

    for u in (1, 2, 3):
        for sign in range(2):
            z_copy(0, 0, u, sign, DISTANCE[u] * (1 - 2 * sign)).start()
    first(0, True)

    def tick(t, carry):
        def run_slot(u, run, also=True):
            @pl.when(jnp.logical_and(jnp.logical_and(u != 0, u != LAST), also))
            def _():
                run(u, False)

            @pl.when(jnp.logical_and(jnp.logical_or(u == 0, u == LAST), also))
            def _():
                run(u, True)

        def when(lag, run):
            run_slot(t - lag, run, jnp.logical_and(t >= lag, t <= LAST + lag))

        @pl.when(t <= LAST + 3)
        def _():
            when(2, third)
            when(3, fourth)

            @pl.when(t <= LAST)
            def _():
                run_slot(t, first)

        slot = jnp.where(t < 10, t - 5, jnp.where(t == 10, 7, jnp.where(t == 13, 8, t - 6)))
        run_slot(slot, score, t >= 5)

        @pl.when(t <= LAST + 4)
        def _():
            when(4, fifth)

        run_slot(slot, collect, t >= 5)
        for u in (7, 8):
            @pl.when(t == 2 * u - 6)
            def _():
                passed(u)

        return carry

    lax.fori_loop(1, 14, tick, 0)
    for t in range(aux // 256):
        cols = slice(t * 256, (t + 1) * 256)
        out[:, :, cols] = acc[:, cols].reshape(occ_dev, local_virt, 256).astype(BF16)

    for ref, sem in (
        (fifteen, rs_send),
        (pieces.at[pl.ds(0, 11)], z_send),
        (ybuf.at[pl.ds(0, 3), 0, 0, pl.ds(0, 3)], a_send),
        (ybuf.at[:, 0, 0], b_send),
        (ybuf.at[pl.ds(0, 4)], c_send),
        (ybuf.at[0], f_send),
    ):
        send(ref, ref, sem, rs_recv, x_at(1)).wait_send()


def per_device(integrals, occ_energy, virt_energy, partners):
    occ_dev, local_virt, aux = integrals.shape
    rows = occ_dev * local_virt
    dma = pltpu.SemaphoreType.DMA
    return pl.pallas_call(
        kernel,
        out_shape=pltpu.VMEM(integrals.shape, BF16),
        in_specs=[
            pl.BlockSpec(memory_space=pl.ANY),
            pl.BlockSpec(memory_space=pl.ANY),
            pl.BlockSpec(memory_space=pl.ANY),
            pl.BlockSpec(memory_space=pl.ANY),
        ],
        out_specs=pl.BlockSpec(memory_space=pltpu.VMEM),
        scratch_shapes=[
            pltpu.SMEM(partners.shape, partners.dtype),
            pltpu.SMEM(occ_energy.shape, F32),
            pltpu.VMEM((8, LANES), F32),
            pltpu.VMEM(integrals.shape, BF16),
            pltpu.VMEM((NOCC_AX, 2, local_virt, LANES), BF16),
            pltpu.VMEM((NOCC_AX, 2, local_virt, LANES), BF16),
            pltpu.VMEM((SLOTS, NC, 2, NY, NX, 2, local_virt, LANES), BF16),
            pltpu.VMEM((rows, aux), F32),
            pltpu.VMEM((rows, 2 * LANES), BF16),
            pltpu.VMEM((rows, LANES), F32),
            pltpu.VMEM((rows, LANES), F32),
            pltpu.VMEM((SLOTS, 8, LANES), F32),
            pltpu.VMEM((2, 8, LANES), F32),
            dma, dma((3,)),
            dma, dma,
            dma, dma((SLOTS,)),
            dma, dma((SLOTS,)),
            dma, dma((SLOTS, 2)),
            dma, dma((SLOTS,)),
            dma, dma((3,)),
        ],
        compiler_params=pltpu.CompilerParams(collective_id=0, has_side_effects=True),
    )(partners, occ_energy, virt_energy.reshape(8, LANES), integrals)


def solution(mesh):
    in_specs = (P("occ", "virt", None), P(), P(), P())
    return jax.shard_map(
        per_device, mesh=mesh, in_specs=in_specs, out_specs=P("occ", "virt", None), check_vma=False
    )
```

```python
import jax
import jax.numpy as jnp
from jax import lax
from jax.experimental import pallas as pl
from jax.experimental.pallas import tpu as pltpu
from jax.sharding import PartitionSpec as P

MESH = pl.DeviceIdType.MESH
BF16, F32 = jnp.bfloat16, jnp.float32
NX, NY, NC, NZ = 4, 4, 2, 16
NOCC_AX = 16
LANES = 128
DISTANCE = (0, 1, 3, 5, 6, 7, 8, 2, 4)
SLOTS = len(DISTANCE)
LAST = 6


def kernel(
    partners_hbm, occ_hbm, virt_hbm, x_hbm, out,
    partners, occ_energy, virt_energy, xv, pieces, got, ybuf, acc, amp, va, own, vb, vh,
    x_sem, e_sem, rs_send, rs_recv, z_send, z_recv,
    a_send, a_recv, b_send, b_recv, c_send, c_recv, f_send, f_recv,
):
    occ_dev, local_virt, aux = xv.shape
    rows = occ_dev * local_virt
    o, v = lax.axis_index("occ"), lax.axis_index("virt")
    x, yh, c = o // 4, (o // 2) % 2, o % 2
    yl, z = v // NZ, v % NZ
    y = 2 * yh + yl
    step_dir = 1 - 2 * c

    def at(xx, yy, cc, zz):
        return {"occ": (xx * 2 + yy // 2) * 2 + cc, "virt": (yy % 2) * NZ + zz}

    def send(src, dst, s_sem, r_sem, device):
        return pltpu.make_async_remote_copy(
            src_ref=src, dst_ref=dst, send_sem=s_sem, recv_sem=r_sem,
            device_id=device, device_id_type=MESH,
        )

    def x_at(d):
        return at((x + d + NX) % NX, y, c, z)

    def y_at(d):
        return at(x, (y + d + NY) % NY, c, z)

    def member(dx, dyh, dc):
        return (((x + dx) % NX) * 2 + (yh + dyh) % 2) * 2 + (c + dc) % 2

    def z_at(d):
        return at(x, y, c, (z + d + NZ) % NZ)

    copies = [
        pltpu.make_async_copy(partners_hbm, partners, e_sem.at[0]),
        pltpu.make_async_copy(occ_hbm, occ_energy, e_sem.at[1]),
        pltpu.make_async_copy(virt_hbm, virt_energy, e_sem.at[2]),
    ]
    third_of = occ_dev // 3
    x_copies = [
        pltpu.make_async_copy(x_hbm.at[pl.ds(i * third_of, third_of)], xv.at[pl.ds(i * third_of, third_of)], x_sem.at[i])
        for i in range(3)
    ]
    for copy in x_copies + copies:
        copy.start()

    barrier = pltpu.get_barrier_semaphore()
    others = [(dx, dyh, dc) for dx, dyh in ((2, 1), (1, 1), (3, 1), (2, 0), (0, 1), (1, 0), (3, 0), (0, 0)) for dc in (0, 1)][:-2] + [(0, 0, 1)]
    peers = [z_at(sign * d) for d in (3, 2) for sign in (1, -1)]
    peers += [{"occ": member(*d), "virt": v} for d in others[:-1]]
    peers += [z_at(1), z_at(-1), y_at(1), y_at(-1), {"occ": member(0, 0, 1), "virt": v}]
    for peer in peers:
        pl.semaphore_signal(barrier, inc=1, device_id=peer, device_id_type=MESH)

    copies[0].wait()
    for copy in x_copies:
        copy.wait()
    for s in range(2):
        block = xv[partners[s] % occ_dev]
        for j in range(NOCC_AX):
            pieces[j, s] = block[:, j * LANES:(j + 1) * LANES]

    pl.semaphore_wait(barrier, len(peers))

    for d in others:
        send(pieces.at[member(*d)], got.at[o], rs_send, rs_recv, {"occ": member(*d), "virt": v}).start()
    got[o] = pieces[o]

    copies[1].wait()
    copies[2].wait()
    lane = lax.broadcasted_iota(jnp.int32, (local_virt, LANES), 1)
    sub = lax.broadcasted_iota(jnp.int32, (local_virt, LANES), 0)
    line = jnp.broadcast_to(virt_energy[pl.ds(v // 4, 1), :], (local_virt, LANES))
    mine = jnp.sum(jnp.where(lane == sub + (v % 4) * local_virt, line, 0.0), axis=1, keepdims=True)
    mine = jnp.broadcast_to(mine, (local_virt, LANES))
    for i in range(occ_dev):
        va[pl.ds(i * local_virt, local_virt), :] = mine
        own[pl.ds(i * local_virt, local_virt), :] = jnp.full((local_virt, LANES), occ_energy[o * occ_dev + i], F32)
    lane8 = lax.broadcasted_iota(jnp.int32, (8, LANES), 1) // 32

    def turned(yy, zz, slot):
        row = jnp.broadcast_to(virt_energy[pl.ds(yy * 4 + zz // 4, 1), :], (8, LANES))
        return pltpu.roll(row, ((slot - zz % 4 + 4) % 4) * 32, 1)

    for u, d in enumerate(DISTANCE):
        if d in (0, NZ // 2):
            continue
        total = jnp.zeros((8, LANES), F32)
        for yy in range(2):
            for sign in range(2):
                zz = (z + d) % NZ if sign else (z + NZ - d) % NZ
                total = jnp.where(lane8 == yy * 2 + sign, turned(yy, zz, yy * 2 + sign), total)
        vb[u] = total
    for h in range(2):
        total = jnp.zeros((8, LANES), F32)
        for s in range(2):
            for yy in range(2):
                total = jnp.where(lane8 == s * 2 + yy, turned(yy, (z + 8 * h) % NZ, s * 2 + yy), total)
        vh[h] = total
    acc[...] = jnp.zeros_like(acc)

    fifteen = pieces.at[pl.ds(0, NOCC_AX - 1)]
    send(fifteen, fifteen, rs_send, rs_recv, x_at(1)).wait_recv()
    for s in range(2):
        ybuf[0, c, s, y, x, 0] = got[partners[s] // occ_dev, s]

    def z_copy(u, source, to, sign, d):
        return send(
            ybuf.at[u, c, :, y, x, source], ybuf.at[to, c, :, y, x, sign], z_send, z_recv.at[to], z_at(d)
        )

    def first(u, half):
        if half:
            @pl.when(u > 0)
            def _():
                ref = pieces.at[0]
                send(ref, ref, z_send, z_recv.at[u], z_at(1)).wait_recv()
        else:
            ref = pieces.at[pl.ds(0, 2)]
            send(ref, ref, z_send, z_recv.at[u], z_at(1)).wait_recv()

            for source, to in ((2, 3), (2, 4), (3, 5), (4, 6)):
                @pl.when(u == source)
                def _():
                    hops = DISTANCE[to] - DISTANCE[source]
                    z_copy(source, 0, to, 0, hops).start()
                    if to < LAST:
                        z_copy(source, 1, to, 1, -hops).start()

        for d in (2, 1, -1):
            for s in range(2):
                ref = ybuf.at[u, c, s, y, x, 0] if half else ybuf.at[u, c, s, y, x]
                send(ref, ref, a_send, a_recv.at[u], (y_at if s else x_at)(d)).start()

    def whole(u, half, s, index):
        if half:
            return ybuf.at[u, c, 1, :, index, 0] if s else ybuf.at[u, c, 0, index, :, 0]
        return ybuf.at[u, c, 1, :, index] if s else ybuf.at[u, c, 0, index]

    def third(u, half):
        six = ybuf.at[0, 0, 0, pl.ds(0, 3), pl.ds(0, 2), 0] if half else ybuf.at[0, 0, 0, pl.ds(0, 3), pl.ds(0, 2)]
        send(six, six, a_send, a_recv.at[u], x_at(1)).wait_recv()
        for s in range(2):
            ref = whole(u, half, s, x if s else y)
            to = x_at if s else y_at
            send(ref, ref, b_send, b_recv.at[u, 0], to(step_dir)).start()
            send(ref, ref, b_send, b_recv.at[u, 1], to(-step_dir)).start()

    def fourth(u, half):
        eight = ybuf.at[0, 0, 0, pl.ds(0, 2), :, 0] if half else ybuf.at[0, 0, 0, pl.ds(0, 2)]
        send(eight, eight, b_send, b_recv.at[u, 0], x_at(1)).wait_recv()
        for s in range(2):
            ref = whole(u, half, s, ((x if s else y) - step_dir + 4) % 4)
            send(ref, ref, b_send, b_recv.at[u, 1], (x_at if s else y_at)(step_dir)).start()

    def twin(u, half, core):
        ref = ybuf.at[u, core, :, :, :, 0] if half else ybuf.at[u, core]
        return send(ref, ref, c_send, c_recv.at[u], at(x, y, 1 - c, z))

    def fifth(u, half):
        sixteen = ybuf.at[0, 0, 0, :, :, 0] if half else ybuf.at[0, 0, 0]
        send(sixteen, sixteen, b_send, b_recv.at[u, 1], x_at(1)).wait_recv()
        twin(u, half, c).start()
        if not half:
            @pl.when(u < 3)
            def _():
                for sign in range(2):
                    send(
                        ybuf.at[u, c, :, :, :, sign], ybuf.at[u + LAST, c, :, :, :, sign],
                        f_send, f_recv.at[u], z_at(1 - 2 * sign),
                    ).start()

    def passed(u):
        send(ybuf.at[0, 0], ybuf.at[0, 0], f_send, f_recv.at[u - LAST], z_at(1)).wait_recv()
        twin(u, False, c).start()

    def tile(u, half, t):
        parts = []
        for s in range(2):
            for yy in range(2):
                halves = []
                for cc in range(2):
                    if half:
                        halves.append(ybuf[u, cc, s, 2 * (t % 2) + yy, t // 2, 0])
                    else:
                        halves.append(ybuf[u, cc, s, 2 * (t % 2) + yy, t // 2].reshape(2 * local_virt, LANES))
                parts.append(jnp.concatenate(halves, axis=1))
        return jnp.concatenate(parts, axis=0)

    def score(u, half):
        twin(u, half, 1 - c).wait_recv()
        width = LANES if half else 2 * LANES
        scores = jnp.zeros((rows, width), F32)
        for t in range(aux // 256):
            left = xv[:, :, t * 256:(t + 1) * 256].reshape(rows, 256)
            scores += lax.dot_general(left, tile(u, half, t), (((1,), (1,)), ((), ())), preferred_element_type=F32)
        line = vh[u // LAST] if half else vb[u]
        base = va[...] + line[0:1, :] - own[...]
        pair = [occ_energy[partners[s]] for s in range(2)]
        if half:
            both = jnp.where(lax.broadcasted_iota(jnp.int32, (1, LANES), 1) < 64, pair[0], pair[1])
            amp[:, :LANES] = (scores / (base - both)).astype(BF16)
        else:
            for s in range(2):
                cols = slice(s * LANES, (s + 1) * LANES)
                amp[:, cols] = (scores[:, cols] / (base - pair[s])).astype(BF16)

    def collect(u, half):
        for t in range(aux // 256):
            cols = slice(t * 256, (t + 1) * 256)
            left = amp[:, :LANES] if half else amp[...]
            acc[:, cols] += jnp.dot(left, tile(u, half, t), preferred_element_type=F32)

    for u in (1, 2):
        for sign in range(2):
            z_copy(0, 0, u, sign, DISTANCE[u] * (1 - 2 * sign)).start()
    first(0, True)

    def tick(t, carry):
        def run_slot(u, run, also=True):
            @pl.when(jnp.logical_and(jnp.logical_and(u != 0, u != LAST), also))
            def _():
                run(u, False)

            @pl.when(jnp.logical_and(jnp.logical_or(u == 0, u == LAST), also))
            def _():
                run(u, True)

        def when(lag, run):
            run_slot(t - lag, run, jnp.logical_and(t >= lag, t <= LAST + lag))

        @pl.when(t <= LAST + 3)
        def _():
            when(2, third)
            when(3, fourth)

            @pl.when(t <= LAST)
            def _():
                run_slot(t, first)

        slot = jnp.where(t < 10, t - 5, jnp.where(t == 10, 7, jnp.where(t == 13, 8, t - 6)))
        run_slot(slot, score, t >= 5)

        @pl.when(t <= LAST + 4)
        def _():
            when(4, fifth)

        run_slot(slot, collect, t >= 5)
        for u in (7, 8):
            @pl.when(t == 2 * u - 6)
            def _():
                passed(u)

        return carry

    lax.fori_loop(1, 14, tick, 0)
    for t in range(aux // 256):
        cols = slice(t * 256, (t + 1) * 256)
        out[:, :, cols] = acc[:, cols].reshape(occ_dev, local_virt, 256).astype(BF16)

    for ref, sem in (
        (fifteen, rs_send),
        (pieces.at[pl.ds(0, 11)], z_send),
        (ybuf.at[pl.ds(0, 3), 0, 0, pl.ds(0, 3)], a_send),
        (ybuf.at[:, 0, 0], b_send),
        (ybuf.at[pl.ds(0, 4)], c_send),
        (ybuf.at[0], f_send),
    ):
        send(ref, ref, sem, rs_recv, x_at(1)).wait_send()


def per_device(integrals, occ_energy, virt_energy, partners):
    occ_dev, local_virt, aux = integrals.shape
    rows = occ_dev * local_virt
    dma = pltpu.SemaphoreType.DMA
    return pl.pallas_call(
        kernel,
        out_shape=pltpu.VMEM(integrals.shape, BF16),
        in_specs=[
            pl.BlockSpec(memory_space=pl.ANY),
            pl.BlockSpec(memory_space=pl.ANY),
            pl.BlockSpec(memory_space=pl.ANY),
            pl.BlockSpec(memory_space=pl.ANY),
        ],
        out_specs=pl.BlockSpec(memory_space=pltpu.VMEM),
        scratch_shapes=[
            pltpu.SMEM(partners.shape, partners.dtype),
            pltpu.SMEM(occ_energy.shape, F32),
            pltpu.VMEM((8, LANES), F32),
            pltpu.VMEM(integrals.shape, BF16),
            pltpu.VMEM((NOCC_AX, 2, local_virt, LANES), BF16),
            pltpu.VMEM((NOCC_AX, 2, local_virt, LANES), BF16),
            pltpu.VMEM((SLOTS, NC, 2, NY, NX, 2, local_virt, LANES), BF16),
            pltpu.VMEM((rows, aux), F32),
            pltpu.VMEM((rows, 2 * LANES), BF16),
            pltpu.VMEM((rows, LANES), F32),
            pltpu.VMEM((rows, LANES), F32),
            pltpu.VMEM((SLOTS, 8, LANES), F32),
            pltpu.VMEM((2, 8, LANES), F32),
            dma((3,)), dma((3,)),
            dma, dma,
            dma, dma((LAST + 1,)),
            dma, dma((LAST + 1,)),
            dma, dma((LAST + 1, 2)),
            dma, dma((SLOTS,)),
            dma, dma((3,)),
        ],
        compiler_params=pltpu.CompilerParams(collective_id=0, has_side_effects=True),
    )(partners, occ_energy, virt_energy.reshape(8, LANES), integrals)


def solution(mesh):
    in_specs = (P("occ", "virt", None), P(), P(), P())
    return jax.shard_map(
        per_device, mesh=mesh, in_specs=in_specs, out_specs=P("occ", "virt", None), check_vma=False
    )
```

```python
import jax
import jax.numpy as jnp
from jax import lax
from jax.experimental import pallas as pl
from jax.experimental.pallas import tpu as pltpu
from jax.sharding import PartitionSpec as P

MESH = pl.DeviceIdType.MESH
BF16, F32 = jnp.bfloat16, jnp.float32
NX, NY, NC, NZ = 4, 4, 2, 16
NOCC_AX = 16
LANES = 128
DISTANCE = (0, 1, 3, 5, 6, 7, 8, 2, 4)
SLOTS = len(DISTANCE)
LAST = 6


def kernel(
    partners_hbm, occ_hbm, virt_hbm, x_hbm, out,
    partners, occ_energy, virt_energy, xv, pieces, got, ybuf, acc, amp, va, own, vb, vh,
    x_sem, e_sem, rs_send, rs_recv, z_send, z_recv,
    a_send, a_recv, b_send, b_recv, c_send, c_recv, f_send, f_recv,
):
    occ_dev, local_virt, aux = xv.shape
    rows = occ_dev * local_virt
    o, v = lax.axis_index("occ"), lax.axis_index("virt")
    x, yh, c = o // 4, (o // 2) % 2, o % 2
    yl, z = v // NZ, v % NZ
    y = 2 * yh + yl
    step_dir = 1 - 2 * c

    def at(xx, yy, cc, zz):
        return {"occ": (xx * 2 + yy // 2) * 2 + cc, "virt": (yy % 2) * NZ + zz}

    def send(src, dst, s_sem, r_sem, device):
        return pltpu.make_async_remote_copy(
            src_ref=src, dst_ref=dst, send_sem=s_sem, recv_sem=r_sem,
            device_id=device, device_id_type=MESH,
        )

    def x_at(d):
        return at((x + d + NX) % NX, y, c, z)

    def y_at(d):
        return at(x, (y + d + NY) % NY, c, z)

    def member(dx, dyh, dc):
        return (((x + dx) % NX) * 2 + (yh + dyh) % 2) * 2 + (c + dc) % 2

    def z_at(d):
        return at(x, y, c, (z + d + NZ) % NZ)

    copies = [
        pltpu.make_async_copy(partners_hbm, partners, e_sem.at[0]),
        pltpu.make_async_copy(occ_hbm, occ_energy, e_sem.at[1]),
        pltpu.make_async_copy(virt_hbm, virt_energy, e_sem.at[2]),
    ]
    third_of = occ_dev // 3
    x_copies = [
        pltpu.make_async_copy(x_hbm.at[pl.ds(i * third_of, third_of)], xv.at[pl.ds(i * third_of, third_of)], x_sem.at[i])
        for i in range(3)
    ]
    for copy in x_copies + copies:
        copy.start()

    barrier = pltpu.get_barrier_semaphore()
    others = [(dx, dyh, dc) for dx, dyh in ((2, 1), (1, 1), (3, 1), (2, 0), (0, 1), (1, 0), (3, 0), (0, 0)) for dc in (0, 1)][:-2] + [(0, 0, 1)]
    peers = [z_at(sign * d) for d in (3, 2) for sign in (1, -1)]
    peers += [{"occ": member(*d), "virt": v} for d in others[:-1]]
    peers += [z_at(1), z_at(-1), y_at(1), y_at(-1), {"occ": member(0, 0, 1), "virt": v}]
    for peer in peers:
        pl.semaphore_signal(barrier, inc=1, device_id=peer, device_id_type=MESH)

    copies[0].wait()
    for copy in x_copies:
        copy.wait()
    for s in range(2):
        block = xv[partners[s] % occ_dev]
        for j in range(NOCC_AX):
            pieces[j, s] = block[:, j * LANES:(j + 1) * LANES]

    pl.semaphore_wait(barrier, len(peers))

    for d in others:
        send(pieces.at[member(*d)], got.at[o], rs_send, rs_recv, {"occ": member(*d), "virt": v}).start()
    got[o] = pieces[o]

    copies[1].wait()
    copies[2].wait()
    lane = lax.broadcasted_iota(jnp.int32, (local_virt, LANES), 1)
    sub = lax.broadcasted_iota(jnp.int32, (local_virt, LANES), 0)
    line = jnp.broadcast_to(virt_energy[pl.ds(v // 4, 1), :], (local_virt, LANES))
    mine = jnp.sum(jnp.where(lane == sub + (v % 4) * local_virt, line, 0.0), axis=1, keepdims=True)
    mine = jnp.broadcast_to(mine, (local_virt, LANES))
    for i in range(occ_dev):
        va[pl.ds(i * local_virt, local_virt), :] = mine
        own[pl.ds(i * local_virt, local_virt), :] = jnp.full((local_virt, LANES), occ_energy[o * occ_dev + i], F32)
    lane8 = lax.broadcasted_iota(jnp.int32, (8, LANES), 1) // 32

    def turned(yy, zz, slot):
        row = jnp.broadcast_to(virt_energy[pl.ds(yy * 4 + zz // 4, 1), :], (8, LANES))
        return pltpu.roll(row, ((slot - zz % 4 + 4) % 4) * 32, 1)

    for u, d in enumerate(DISTANCE):
        if d in (0, NZ // 2):
            continue
        total = jnp.zeros((8, LANES), F32)
        for yy in range(2):
            for sign in range(2):
                zz = (z + d) % NZ if sign else (z + NZ - d) % NZ
                total = jnp.where(lane8 == yy * 2 + sign, turned(yy, zz, yy * 2 + sign), total)
        vb[u] = total
    for h in range(2):
        total = jnp.zeros((8, LANES), F32)
        for s in range(2):
            for yy in range(2):
                total = jnp.where(lane8 == s * 2 + yy, turned(yy, (z + 8 * h) % NZ, s * 2 + yy), total)
        vh[h] = total
    acc[...] = jnp.zeros_like(acc)

    fifteen = pieces.at[pl.ds(0, NOCC_AX - 1)]
    send(fifteen, fifteen, rs_send, rs_recv, x_at(1)).wait_recv()
    for s in range(2):
        ybuf[0, c, s, y, x, 0] = got[partners[s] // occ_dev, s]

    def z_copy(u, source, to, sign, d):
        return send(
            ybuf.at[u, c, :, y, x, source], ybuf.at[to, c, :, y, x, sign], z_send, z_recv.at[to], z_at(d)
        )

    def first(u, half):
        if half:
            @pl.when(u > 0)
            def _():
                ref = pieces.at[0]
                send(ref, ref, z_send, z_recv.at[u], z_at(1)).wait_recv()
        else:
            ref = pieces.at[pl.ds(0, 2)]
            send(ref, ref, z_send, z_recv.at[u], z_at(1)).wait_recv()

            for source, to in ((2, 3), (2, 4), (3, 5), (4, 6)):
                @pl.when(u == source)
                def _():
                    hops = DISTANCE[to] - DISTANCE[source]
                    z_copy(source, 0, to, 0, hops).start()
                    if to < LAST:
                        z_copy(source, 1, to, 1, -hops).start()

        for d in (2, 1, -1):
            for s in range(2):
                ref = ybuf.at[u, c, s, y, x, 0] if half else ybuf.at[u, c, s, y, x]
                send(ref, ref, a_send, a_recv.at[u], (y_at if s else x_at)(d)).start()

    def whole(u, half, s, index):
        if half:
            return ybuf.at[u, c, 1, :, index, 0] if s else ybuf.at[u, c, 0, index, :, 0]
        return ybuf.at[u, c, 1, :, index] if s else ybuf.at[u, c, 0, index]

    def third(u, half):
        six = ybuf.at[0, 0, 0, pl.ds(0, 3), pl.ds(0, 2), 0] if half else ybuf.at[0, 0, 0, pl.ds(0, 3), pl.ds(0, 2)]
        send(six, six, a_send, a_recv.at[u], x_at(1)).wait_recv()
        for s in range(2):
            ref = whole(u, half, s, x if s else y)
            to = x_at if s else y_at
            send(ref, ref, b_send, b_recv.at[u, 0], to(step_dir)).start()
            send(ref, ref, b_send, b_recv.at[u, 1], to(-step_dir)).start()

    def fourth(u, half):
        eight = ybuf.at[0, 0, 0, pl.ds(0, 2), :, 0] if half else ybuf.at[0, 0, 0, pl.ds(0, 2)]
        send(eight, eight, b_send, b_recv.at[u, 0], x_at(1)).wait_recv()
        for s in range(2):
            ref = whole(u, half, s, ((x if s else y) - step_dir + 4) % 4)
            send(ref, ref, b_send, b_recv.at[u, 1], (x_at if s else y_at)(step_dir)).start()

    def twin(u, half, core):
        ref = ybuf.at[u, core, :, :, :, 0] if half else ybuf.at[u, core]
        return send(ref, ref, c_send, c_recv.at[u], at(x, y, 1 - c, z))

    def fifth(u, half):
        sixteen = ybuf.at[0, 0, 0, :, :, 0] if half else ybuf.at[0, 0, 0]
        send(sixteen, sixteen, b_send, b_recv.at[u, 1], x_at(1)).wait_recv()
        twin(u, half, c).start()
        if not half:
            @pl.when(u < 3)
            def _():
                for sign in range(2):
                    send(
                        ybuf.at[u, c, :, :, :, sign], ybuf.at[u + LAST, c, :, :, :, sign],
                        f_send, f_recv.at[u], z_at(1 - 2 * sign),
                    ).start()

    def passed(u):
        send(ybuf.at[0, 0], ybuf.at[0, 0], f_send, f_recv.at[u - LAST], z_at(1)).wait_recv()
        twin(u, False, c).start()

    def tile(u, half, t):
        parts = []
        for s in range(2):
            for yy in range(2):
                halves = []
                for cc in range(2):
                    if half:
                        halves.append(ybuf[u, cc, s, 2 * (t % 2) + yy, t // 2, 0])
                    else:
                        halves.append(ybuf[u, cc, s, 2 * (t % 2) + yy, t // 2].reshape(2 * local_virt, LANES))
                parts.append(jnp.concatenate(halves, axis=1))
        return jnp.concatenate(parts, axis=0)

    def score(u, half):
        twin(u, half, 1 - c).wait_recv()
        width = LANES if half else 2 * LANES
        scores = jnp.zeros((rows, width), F32)
        for t in range(aux // 256):
            left = xv[:, :, t * 256:(t + 1) * 256].reshape(rows, 256)
            scores += lax.dot_general(left, tile(u, half, t), (((1,), (1,)), ((), ())), preferred_element_type=F32)
        line = vh[u // LAST] if half else vb[u]
        base = va[...] + line[0:1, :] - own[...]
        pair = [occ_energy[partners[s]] for s in range(2)]
        if half:
            both = jnp.where(lax.broadcasted_iota(jnp.int32, (1, LANES), 1) < 64, pair[0], pair[1])
            amp[:, :LANES] = (scores / (base - both)).astype(BF16)
        else:
            for s in range(2):
                cols = slice(s * LANES, (s + 1) * LANES)
                amp[:, cols] = (scores[:, cols] / (base - pair[s])).astype(BF16)

    def collect(u, half):
        for t in range(aux // 256):
            cols = slice(t * 256, (t + 1) * 256)
            left = amp[:, :LANES] if half else amp[...]
            acc[:, cols] += jnp.dot(left, tile(u, half, t), preferred_element_type=F32)

    for u in (1, 2):
        for sign in range(2):
            z_copy(0, 0, u, sign, DISTANCE[u] * (1 - 2 * sign)).start()
    first(0, True)

    def tick(t, carry):
        def run_slot(u, run, also=True):
            @pl.when(jnp.logical_and(jnp.logical_and(u != 0, u != LAST), also))
            def _():
                run(u, False)

            @pl.when(jnp.logical_and(jnp.logical_or(u == 0, u == LAST), also))
            def _():
                run(u, True)

        def when(lag, run):
            run_slot(t - lag, run, jnp.logical_and(t >= lag, t <= LAST + lag))

        @pl.when(t <= LAST + 3)
        def _():
            when(2, third)
            run_slot(t - 3, fourth, jnp.logical_and(t >= 3, t < LAST + 3))

            @pl.when(t <= LAST)
            def _():
                run_slot(t, first)

        slot = jnp.where(t < 10, t - 5, jnp.where(t == 10, 7, jnp.where(t == 13, 8, t - 6)))
        run_slot(slot, score, t >= 5)

        @pl.when(t == LAST + 3)
        def _():
            fourth(LAST, True)

        @pl.when(t <= LAST + 4)
        def _():
            when(4, fifth)

        run_slot(slot, collect, t >= 5)
        for u in (7, 8):
            @pl.when(t == 2 * u - 6)
            def _():
                passed(u)

        return carry

    lax.fori_loop(1, 14, tick, 0)
    for t in range(aux // 256):
        cols = slice(t * 256, (t + 1) * 256)
        out[:, :, cols] = acc[:, cols].reshape(occ_dev, local_virt, 256).astype(BF16)

    for ref, sem in (
        (fifteen, rs_send),
        (pieces.at[pl.ds(0, 11)], z_send),
        (ybuf.at[pl.ds(0, 3), 0, 0, pl.ds(0, 3)], a_send),
        (ybuf.at[:, 0, 0], b_send),
        (ybuf.at[pl.ds(0, 4)], c_send),
        (ybuf.at[0], f_send),
    ):
        send(ref, ref, sem, rs_recv, x_at(1)).wait_send()


def per_device(integrals, occ_energy, virt_energy, partners):
    occ_dev, local_virt, aux = integrals.shape
    rows = occ_dev * local_virt
    dma = pltpu.SemaphoreType.DMA
    return pl.pallas_call(
        kernel,
        out_shape=pltpu.VMEM(integrals.shape, BF16),
        in_specs=[
            pl.BlockSpec(memory_space=pl.ANY),
            pl.BlockSpec(memory_space=pl.ANY),
            pl.BlockSpec(memory_space=pl.ANY),
            pl.BlockSpec(memory_space=pl.ANY),
        ],
        out_specs=pl.BlockSpec(memory_space=pltpu.VMEM),
        scratch_shapes=[
            pltpu.SMEM(partners.shape, partners.dtype),
            pltpu.SMEM(occ_energy.shape, F32),
            pltpu.VMEM((8, LANES), F32),
            pltpu.VMEM(integrals.shape, BF16),
            pltpu.VMEM((NOCC_AX, 2, local_virt, LANES), BF16),
            pltpu.VMEM((NOCC_AX, 2, local_virt, LANES), BF16),
            pltpu.VMEM((SLOTS, NC, 2, NY, NX, 2, local_virt, LANES), BF16),
            pltpu.VMEM((rows, aux), F32),
            pltpu.VMEM((rows, 2 * LANES), BF16),
            pltpu.VMEM((rows, LANES), F32),
            pltpu.VMEM((rows, LANES), F32),
            pltpu.VMEM((SLOTS, 8, LANES), F32),
            pltpu.VMEM((2, 8, LANES), F32),
            dma((3,)), dma((3,)),
            dma, dma,
            dma, dma((LAST + 1,)),
            dma, dma((LAST + 1,)),
            dma, dma((LAST + 1, 2)),
            dma, dma((SLOTS,)),
            dma, dma((3,)),
        ],
        compiler_params=pltpu.CompilerParams(collective_id=0, has_side_effects=True),
    )(partners, occ_energy, virt_energy.reshape(8, LANES), integrals)


def solution(mesh):
    in_specs = (P("occ", "virt", None), P(), P(), P())
    return jax.shard_map(
        per_device, mesh=mesh, in_specs=in_specs, out_specs=P("occ", "virt", None), check_vma=False
    )
```

```python
import jax
import jax.numpy as jnp
from jax import lax
from jax.experimental import pallas as pl
from jax.experimental.pallas import tpu as pltpu
from jax.sharding import PartitionSpec as P

MESH = pl.DeviceIdType.MESH
BF16, F32 = jnp.bfloat16, jnp.float32
NX, NY, NC, NZ = 4, 4, 2, 16
NOCC_AX = 16
LANES = 128
DISTANCE = (0, 1, 3, 5, 6, 7, 8, 2, 4)
SLOTS = len(DISTANCE)
LAST = 6


def kernel(
    partners_hbm, occ_hbm, virt_hbm, x_hbm, out,
    partners, occ_energy, virt_energy, xv, pieces, got, ybuf, acc, amp, va, own, vb, vh,
    x_sem, e_sem, rs_send, rs_recv, z_send, z_recv,
    a_send, a_recv, b_send, b_recv, c_send, c_recv, f_send, f_recv,
):
    occ_dev, local_virt, aux = xv.shape
    rows = occ_dev * local_virt
    o, v = lax.axis_index("occ"), lax.axis_index("virt")
    x, yh, c = o // 4, (o // 2) % 2, o % 2
    yl, z = v // NZ, v % NZ
    y = 2 * yh + yl
    step_dir = 1 - 2 * c

    def at(xx, yy, cc, zz):
        return {"occ": (xx * 2 + yy // 2) * 2 + cc, "virt": (yy % 2) * NZ + zz}

    def send(src, dst, s_sem, r_sem, device):
        return pltpu.make_async_remote_copy(
            src_ref=src, dst_ref=dst, send_sem=s_sem, recv_sem=r_sem,
            device_id=device, device_id_type=MESH,
        )

    def x_at(d):
        return at((x + d + NX) % NX, y, c, z)

    def y_at(d):
        return at(x, (y + d + NY) % NY, c, z)

    def member(dx, dyh, dc):
        return (((x + dx) % NX) * 2 + (yh + dyh) % 2) * 2 + (c + dc) % 2

    def z_at(d):
        return at(x, y, c, (z + d + NZ) % NZ)

    copies = [
        pltpu.make_async_copy(partners_hbm, partners, e_sem.at[0]),
        pltpu.make_async_copy(occ_hbm, occ_energy, e_sem.at[1]),
        pltpu.make_async_copy(virt_hbm, virt_energy, e_sem.at[2]),
    ]
    third_of = occ_dev // 3
    x_copies = [
        pltpu.make_async_copy(x_hbm.at[pl.ds(i * third_of, third_of)], xv.at[pl.ds(i * third_of, third_of)], x_sem.at[i])
        for i in range(3)
    ]
    for copy in x_copies + copies:
        copy.start()

    barrier = pltpu.get_barrier_semaphore()
    others = [(dx, dyh, dc) for dx, dyh in ((2, 1), (1, 1), (3, 1), (2, 0), (0, 1), (1, 0), (3, 0), (0, 0)) for dc in (0, 1)][:-2] + [(0, 0, 1)]
    peers = [z_at(sign * d) for d in (4, 3, 2) for sign in (1, -1)]
    peers += [{"occ": member(*d), "virt": v} for d in others[:-1]]
    peers += [z_at(1), z_at(-1), y_at(1), y_at(-1), {"occ": member(0, 0, 1), "virt": v}]
    for peer in peers:
        pl.semaphore_signal(barrier, inc=1, device_id=peer, device_id_type=MESH)

    copies[0].wait()
    for copy in x_copies:
        copy.wait()
    for s in range(2):
        block = xv[partners[s] % occ_dev]
        for j in range(NOCC_AX):
            pieces[j, s] = block[:, j * LANES:(j + 1) * LANES]

    pl.semaphore_wait(barrier, len(peers))

    for d in others:
        send(pieces.at[member(*d)], got.at[o], rs_send, rs_recv, {"occ": member(*d), "virt": v}).start()
    got[o] = pieces[o]

    copies[1].wait()
    copies[2].wait()
    lane = lax.broadcasted_iota(jnp.int32, (local_virt, LANES), 1)
    sub = lax.broadcasted_iota(jnp.int32, (local_virt, LANES), 0)
    line = jnp.broadcast_to(virt_energy[pl.ds(v // 4, 1), :], (local_virt, LANES))
    mine = jnp.sum(jnp.where(lane == sub + (v % 4) * local_virt, line, 0.0), axis=1, keepdims=True)
    mine = jnp.broadcast_to(mine, (local_virt, LANES))
    for i in range(occ_dev):
        va[pl.ds(i * local_virt, local_virt), :] = mine
        own[pl.ds(i * local_virt, local_virt), :] = jnp.full((local_virt, LANES), occ_energy[o * occ_dev + i], F32)
    lane8 = lax.broadcasted_iota(jnp.int32, (8, LANES), 1) // 32

    def turned(yy, zz, slot):
        row = jnp.broadcast_to(virt_energy[pl.ds(yy * 4 + zz // 4, 1), :], (8, LANES))
        return pltpu.roll(row, ((slot - zz % 4 + 4) % 4) * 32, 1)

    for u, d in enumerate(DISTANCE):
        if d in (0, NZ // 2):
            continue
        total = jnp.zeros((8, LANES), F32)
        for yy in range(2):
            for sign in range(2):
                zz = (z + d) % NZ if sign else (z + NZ - d) % NZ
                total = jnp.where(lane8 == yy * 2 + sign, turned(yy, zz, yy * 2 + sign), total)
        vb[u] = total
    for h in range(2):
        total = jnp.zeros((8, LANES), F32)
        for s in range(2):
            for yy in range(2):
                total = jnp.where(lane8 == s * 2 + yy, turned(yy, (z + 8 * h) % NZ, s * 2 + yy), total)
        vh[h] = total
    acc[...] = jnp.zeros_like(acc)

    fifteen = pieces.at[pl.ds(0, NOCC_AX - 1)]
    send(fifteen, fifteen, rs_send, rs_recv, x_at(1)).wait_recv()
    for s in range(2):
        ybuf[0, c, s, y, x, 0] = got[partners[s] // occ_dev, s]

    def z_copy(u, source, to, sign, d):
        return send(
            ybuf.at[u, c, :, y, x, source], ybuf.at[to, c, :, y, x, sign], z_send, z_recv.at[to], z_at(d)
        )

    def first(u, half):
        if half:
            @pl.when(u > 0)
            def _():
                ref = pieces.at[0]
                send(ref, ref, z_send, z_recv.at[u], z_at(1)).wait_recv()
        else:
            ref = pieces.at[pl.ds(0, 2)]
            send(ref, ref, z_send, z_recv.at[u], z_at(1)).wait_recv()

            for source, to in ((1, 3), (2, 4), (3, 5), (4, 6)):
                @pl.when(u == source)
                def _():
                    hops = DISTANCE[to] - DISTANCE[source]
                    z_copy(source, 0, to, 0, hops).start()
                    if to < LAST:
                        z_copy(source, 1, to, 1, -hops).start()

        for d in (2, 1, -1):
            for s in range(2):
                ref = ybuf.at[u, c, s, y, x, 0] if half else ybuf.at[u, c, s, y, x]
                send(ref, ref, a_send, a_recv.at[u], (y_at if s else x_at)(d)).start()

    def whole(u, half, s, index):
        if half:
            return ybuf.at[u, c, 1, :, index, 0] if s else ybuf.at[u, c, 0, index, :, 0]
        return ybuf.at[u, c, 1, :, index] if s else ybuf.at[u, c, 0, index]

    def third(u, half):
        six = ybuf.at[0, 0, 0, pl.ds(0, 3), pl.ds(0, 2), 0] if half else ybuf.at[0, 0, 0, pl.ds(0, 3), pl.ds(0, 2)]
        send(six, six, a_send, a_recv.at[u], x_at(1)).wait_recv()
        for s in range(2):
            ref = whole(u, half, s, x if s else y)
            to = x_at if s else y_at
            send(ref, ref, b_send, b_recv.at[u, 0], to(step_dir)).start()
            send(ref, ref, b_send, b_recv.at[u, 1], to(-step_dir)).start()

    def fourth(u, half):
        eight = ybuf.at[0, 0, 0, pl.ds(0, 2), :, 0] if half else ybuf.at[0, 0, 0, pl.ds(0, 2)]
        send(eight, eight, b_send, b_recv.at[u, 0], x_at(1)).wait_recv()
        for s in range(2):
            ref = whole(u, half, s, ((x if s else y) - step_dir + 4) % 4)
            send(ref, ref, b_send, b_recv.at[u, 1], (x_at if s else y_at)(step_dir)).start()

    def twin(u, half, core):
        ref = ybuf.at[u, core, :, :, :, 0] if half else ybuf.at[u, core]
        return send(ref, ref, c_send, c_recv.at[u], at(x, y, 1 - c, z))

    def fifth(u, half):
        sixteen = ybuf.at[0, 0, 0, :, :, 0] if half else ybuf.at[0, 0, 0]
        send(sixteen, sixteen, b_send, b_recv.at[u, 1], x_at(1)).wait_recv()
        twin(u, half, c).start()
        if not half:
            @pl.when(u < 3)
            def _():
                for sign in range(2):
                    send(
                        ybuf.at[u, c, :, :, :, sign], ybuf.at[u + LAST, c, :, :, :, sign],
                        f_send, f_recv.at[u], z_at(1 - 2 * sign),
                    ).start()

    def passed(u):
        send(ybuf.at[0, 0], ybuf.at[0, 0], f_send, f_recv.at[u - LAST], z_at(1)).wait_recv()
        twin(u, False, c).start()

    def tile(u, half, t):
        parts = []
        for s in range(2):
            for yy in range(2):
                halves = []
                for cc in range(2):
                    if half:
                        halves.append(ybuf[u, cc, s, 2 * (t % 2) + yy, t // 2, 0])
                    else:
                        halves.append(ybuf[u, cc, s, 2 * (t % 2) + yy, t // 2].reshape(2 * local_virt, LANES))
                parts.append(jnp.concatenate(halves, axis=1))
        return jnp.concatenate(parts, axis=0)

    def score(u, half):
        twin(u, half, 1 - c).wait_recv()
        width = LANES if half else 2 * LANES
        scores = jnp.zeros((rows, width), F32)
        for t in range(aux // 256):
            left = xv[:, :, t * 256:(t + 1) * 256].reshape(rows, 256)
            scores += lax.dot_general(left, tile(u, half, t), (((1,), (1,)), ((), ())), preferred_element_type=F32)
        line = vh[u // LAST] if half else vb[u]
        base = va[...] + line[0:1, :] - own[...]
        pair = [occ_energy[partners[s]] for s in range(2)]
        if half:
            both = jnp.where(lax.broadcasted_iota(jnp.int32, (1, LANES), 1) < 64, pair[0], pair[1])
            amp[:, :LANES] = (scores / (base - both)).astype(BF16)
        else:
            for s in range(2):
                cols = slice(s * LANES, (s + 1) * LANES)
                amp[:, cols] = (scores[:, cols] / (base - pair[s])).astype(BF16)

    def collect(u, half):
        for t in range(aux // 256):
            cols = slice(t * 256, (t + 1) * 256)
            left = amp[:, :LANES] if half else amp[...]
            acc[:, cols] += jnp.dot(left, tile(u, half, t), preferred_element_type=F32)

    for u in (1, 2):
        for sign in range(2):
            z_copy(0, 0, u, sign, DISTANCE[u] * (1 - 2 * sign)).start()
    first(0, True)

    def tick(t, carry):
        def run_slot(u, run, also=True):
            @pl.when(jnp.logical_and(jnp.logical_and(u != 0, u != LAST), also))
            def _():
                run(u, False)

            @pl.when(jnp.logical_and(jnp.logical_or(u == 0, u == LAST), also))
            def _():
                run(u, True)

        def when(lag, run):
            run_slot(t - lag, run, jnp.logical_and(t >= lag, t <= LAST + lag))

        @pl.when(t <= LAST + 3)
        def _():
            when(2, third)
            when(3, fourth)

            @pl.when(t <= LAST)
            def _():
                run_slot(t, first)

        slot = jnp.where(t < 10, t - 5, jnp.where(t == 10, 7, jnp.where(t == 13, 8, t - 6)))
        run_slot(slot, score, t >= 5)

        @pl.when(t <= LAST + 4)
        def _():
            when(4, fifth)

        run_slot(slot, collect, t >= 5)
        for u in (7, 8):
            @pl.when(t == 2 * u - 6)
            def _():
                passed(u)

        return carry

    lax.fori_loop(1, 14, tick, 0)
    for t in range(aux // 256):
        cols = slice(t * 256, (t + 1) * 256)
        out[:, :, cols] = acc[:, cols].reshape(occ_dev, local_virt, 256).astype(BF16)

    for ref, sem in (
        (fifteen, rs_send),
        (pieces.at[pl.ds(0, 11)], z_send),
        (ybuf.at[pl.ds(0, 3), 0, 0, pl.ds(0, 3)], a_send),
        (ybuf.at[:, 0, 0], b_send),
        (ybuf.at[pl.ds(0, 4)], c_send),
        (ybuf.at[0], f_send),
    ):
        send(ref, ref, sem, rs_recv, x_at(1)).wait_send()


def per_device(integrals, occ_energy, virt_energy, partners):
    occ_dev, local_virt, aux = integrals.shape
    rows = occ_dev * local_virt
    dma = pltpu.SemaphoreType.DMA
    return pl.pallas_call(
        kernel,
        out_shape=pltpu.VMEM(integrals.shape, BF16),
        in_specs=[
            pl.BlockSpec(memory_space=pl.ANY),
            pl.BlockSpec(memory_space=pl.ANY),
            pl.BlockSpec(memory_space=pl.ANY),
            pl.BlockSpec(memory_space=pl.ANY),
        ],
        out_specs=pl.BlockSpec(memory_space=pltpu.VMEM),
        scratch_shapes=[
            pltpu.SMEM(partners.shape, partners.dtype),
            pltpu.SMEM(occ_energy.shape, F32),
            pltpu.VMEM((8, LANES), F32),
            pltpu.VMEM(integrals.shape, BF16),
            pltpu.VMEM((NOCC_AX, 2, local_virt, LANES), BF16),
            pltpu.VMEM((NOCC_AX, 2, local_virt, LANES), BF16),
            pltpu.VMEM((SLOTS, NC, 2, NY, NX, 2, local_virt, LANES), BF16),
            pltpu.VMEM((rows, aux), F32),
            pltpu.VMEM((rows, 2 * LANES), BF16),
            pltpu.VMEM((rows, LANES), F32),
            pltpu.VMEM((rows, LANES), F32),
            pltpu.VMEM((SLOTS, 8, LANES), F32),
            pltpu.VMEM((2, 8, LANES), F32),
            dma((3,)), dma((3,)),
            dma, dma,
            dma, dma((LAST + 1,)),
            dma, dma((LAST + 1,)),
            dma, dma((LAST + 1, 2)),
            dma, dma((SLOTS,)),
            dma, dma((3,)),
        ],
        compiler_params=pltpu.CompilerParams(collective_id=0, has_side_effects=True),
    )(partners, occ_energy, virt_energy.reshape(8, LANES), integrals)


def solution(mesh):
    in_specs = (P("occ", "virt", None), P(), P(), P())
    return jax.shard_map(
        per_device, mesh=mesh, in_specs=in_specs, out_specs=P("occ", "virt", None), check_vma=False
    )
```
